32 devices in a mesh: grp: 2 (over y), tm: 4 (over z), chan: 4 (over x, core).
Axes of the slice: x: 2, y: 2, z: 4, core: 2. Of those that a mesh axis runs over, the one named last changes fastest.
Arguments:
- voltages: int32 [512, 65536], P(('grp', 'chan'), 'tm'), parts along dimension 0, may hold values from -128 to 127
- beam_delays: int32 [256, 256], replicated, may hold values from 0 to 4095
- cal_gains: float32 [2, 4096, 256], P(None, ('grp', 'tm', 'chan')), parts along dimension 1, may hold values from -4 to 4
Outputs:
- visibilities: bfloat16 [2, 4096, 256, 256], P(None, ('grp', 'tm', 'chan')), parts along dimension 1
- beam_power: bfloat16 [4096, 16, 256], P(('grp', 'tm', 'chan')), parts along dimension 0
The draws below stay inside these ranges and needn't reach their ends.
There are 2 independent parts, one for each index of `grp`. The reference program is written for one: setup_inputs(seed, part) draws one part's arguments, and reference() takes and returns one part's arrays. A program takes and returns all parts, laid end to end along the dimension named above; an argument that names none is the same for every part. Nothing has to cross between parts.
All inputs are finite; a program needn't handle non-finite values.
Results may differ from the reference program's by a relative error of at most 0.0062.
Values may be sent and summed in bfloat16 or wider, within the bound.
A program may use at most 192 MiB of HBM per device.

```python
import math
import jax
import jax.numpy as jnp
from jax import lax

INP = 256
BEAMS = 256
TAPS = 4
SPEC_DEV = 4
NFFT = 4096
CH = 2048
SAMPLES = 65536
N_TM = 4


def plant(values, key, low, high):
    shape = values.shape
    place = [jax.random.randint(jax.random.fold_in(key, axis), (), 0, shape[axis]) for axis in range(len(shape))]
    values = values.at[tuple(place)].set(low)
    longest = shape.index(max(shape))
    place[longest] = (place[longest] + 1) % shape[longest]
    return values.at[tuple(place)].set(high)


def shard_levels(rng, shape, pieces, low, high):
    def one(axis_at, blocks):
        heights = jax.random.uniform(jax.random.fold_in(jax.random.fold_in(rng, 6), axis_at), (blocks,), jnp.float32, low / len(pieces), high / len(pieces))
        return jnp.repeat(jnp.exp(heights), shape[axis_at] // blocks).reshape((-1,) + (1,) * (len(shape) - axis_at - 1))

    factor_of = one(*pieces[0])
    for cut in pieces[1:]:
        factor_of = factor_of * one(*cut)
    return factor_of


def noise(rng, extent, deviation, bound, pieces=(), kind=jnp.bfloat16):
    values = deviation * jax.random.normal(rng, extent, jnp.float32)
    if pieces:
        values = values * shard_levels(rng, extent, pieces, -0.22, 0.18)
    return jnp.clip(values, -bound, bound).astype(kind)


def setup_inputs(seed: int = 0, part: int = 0) -> dict:
    key_list = jax.random.split(jax.random.key(seed), 4)
    own_keys = jax.random.split(jax.random.fold_in(key_list[3], part), 4)
    voltages = plant(jax.random.randint(own_keys[0], (INP, SAMPLES), -128, 128), jax.random.fold_in(own_keys[0], 1), -128, 127).astype(jnp.int32)
    beam_delays = plant(jax.random.randint(key_list[1], (BEAMS, INP), 0, NFFT), jax.random.fold_in(key_list[1], 1), 0, NFFT - 1).astype(jnp.int32)
    cal_gains = noise(own_keys[2], (2, CH, INP), 0.7, 4.0, ((1, 16),), jnp.float32)
    return dict(voltages=voltages, beam_delays=beam_delays, cal_gains=cal_gains)


def pfb_window():
    total_len = TAPS * NFFT
    sample_pos = jnp.arange(total_len, dtype=jnp.float32)
    centre = (sample_pos - total_len / 2 + 0.5) / NFFT
    taper_win = 0.5 - 0.5 * jnp.cos(2.0 * math.pi * (sample_pos + 0.5) / total_len)
    coeffs = jnp.sinc(centre) * taper_win
    coeffs = coeffs / jnp.sqrt(jnp.sum(coeffs * coeffs))
    return coeffs.reshape(TAPS, NFFT)

def reference(voltages, beam_delays, cal_gains):
    spectra_total = SPEC_DEV * N_TM
    coeffs = pfb_window()
    samples = voltages.astype(jnp.float32).reshape(INP, spectra_total, NFFT)
    padded = jnp.concatenate([samples, jnp.zeros((INP, TAPS - 1, NFFT), jnp.float32)], axis=1)
    in_block = 16
    padded = padded.reshape(INP // in_block, in_block, spectra_total + TAPS - 1, NFFT)

    def channelize(block_in):
        filtered = coeffs[0] * block_in[:, 0:spectra_total]
        for tap_index in range(1, TAPS):
            filtered = filtered + coeffs[tap_index] * block_in[:, tap_index:tap_index + spectra_total]
        freq = jnp.fft.rfft(filtered, axis=-1)[..., :CH] * (1.0 / 64.0)
        return (jnp.real(freq).astype(jnp.bfloat16), jnp.imag(freq).astype(jnp.bfloat16))
    spec_re, spec_im = lax.map(channelize, padded)
    spec_re = spec_re.reshape(INP, spectra_total, CH).transpose(2, 1, 0)
    spec_im = spec_im.reshape(INP, spectra_total, CH).transpose(2, 1, 0)
    ch_block = 64
    n_blocks = CH // ch_block
    chan_index = jnp.arange(CH, dtype=jnp.int32).reshape(n_blocks, ch_block)
    weight_norm = 1.0 / math.sqrt(INP)

    def correlate(packed):
        z_re, z_im, g_re, g_im, chan_ids = packed
        a_re = z_re.astype(jnp.float32)
        a_im = z_im.astype(jnp.float32)
        g_re = g_re[:, None, :]
        g_im = g_im[:, None, :]
        cal_re = (g_re * a_re - g_im * a_im).astype(jnp.bfloat16).astype(jnp.float32)
        cal_im = (g_re * a_im + g_im * a_re).astype(jnp.bfloat16).astype(jnp.float32)
        stacked = jnp.concatenate([cal_re, cal_im], axis=1)
        flipped = jnp.concatenate([cal_im, -cal_re], axis=1)
        vis_re = jnp.einsum('ctp,ctq->cpq', stacked, stacked)
        vis_im = jnp.einsum('ctp,ctq->cpq', flipped, stacked)
        vis_out = (jnp.stack([vis_re, vis_im]) / spectra_total).astype(jnp.bfloat16)
        phase_idx = beam_delays[None, :, :] * chan_ids[:, None, None] % NFFT
        angles = phase_idx.astype(jnp.float32) * (2.0 * math.pi / NFFT)
        weight_re = (jnp.cos(angles) * weight_norm).astype(jnp.bfloat16).astype(jnp.float32)
        weight_im = (-jnp.sin(angles) * weight_norm).astype(jnp.bfloat16).astype(jnp.float32)
        beam_re = jnp.einsum('cti,cbi->ctb', cal_re, weight_re) - jnp.einsum('cti,cbi->ctb', cal_im, weight_im)
        beam_im = jnp.einsum('cti,cbi->ctb', cal_im, weight_re) + jnp.einsum('cti,cbi->ctb', cal_re, weight_im)
        power_out = (beam_re * beam_re + beam_im * beam_im).astype(jnp.bfloat16)
        return (vis_out, power_out)
    vis_all, power_all = lax.map(correlate, (spec_re.reshape(n_blocks, ch_block, spectra_total, INP), spec_im.reshape(n_blocks, ch_block, spectra_total, INP), cal_gains[0].reshape(n_blocks, ch_block, INP), cal_gains[1].reshape(n_blocks, ch_block, INP), chan_index))
    visibilities = vis_all.transpose(1, 0, 2, 3, 4).reshape(2, CH, INP, INP)
    beam_power = power_all.reshape(CH, spectra_total, BEAMS)
    return (visibilities, beam_power)
```

```python
import functools
import math

import jax
import jax.numpy as jnp
from jax import lax
from jax.experimental import pallas as pl
from jax.experimental.pallas import tpu as pltpu
from jax.sharding import PartitionSpec as P

TAPS = 4
FA = 64
FB = 64
NFFT = 4096
CH = 2048


def shifted(block, axis, distance):
    devices = range(lax.axis_size(axis))
    route = [(i - distance, i) for i in devices if i - distance in devices]
    return lax.ppermute(block, axis, route)


def pfb_window():
    total_len = TAPS * NFFT
    sample_pos = jnp.arange(total_len, dtype=jnp.float32)
    centre = (sample_pos - total_len / 2 + 0.5) / NFFT
    taper_win = 0.5 - 0.5 * jnp.cos(2.0 * math.pi * (sample_pos + 0.5) / total_len)
    coeffs = jnp.sinc(centre) * taper_win
    coeffs = coeffs / jnp.sqrt(jnp.sum(coeffs * coeffs))
    return coeffs.reshape(TAPS, NFFT)


def phase_table(left, right, modulus):
    phase_idx = left[:, None] * right[None, :] % modulus
    angles = phase_idx.astype(jnp.float32) * (2.0 * math.pi / modulus)
    return (jnp.cos(angles), jnp.sin(angles))


def transform(row_block):
    best = lax.Precision.HIGHEST
    first_idx = jnp.arange(FA, dtype=jnp.int32)
    second_idx = jnp.arange(FB, dtype=jnp.int32)
    half_idx = jnp.arange(FB // 2, dtype=jnp.int32)
    cos_one, sin_one = phase_table(first_idx, first_idx, FA)
    section_re = jnp.einsum("rab,ak->rkb", row_block, cos_one, precision=best)
    section_im = -jnp.einsum("rab,ak->rkb", row_block, sin_one, precision=best)
    twid_cos, twid_sin = phase_table(first_idx, second_idx, NFFT)
    inner_re = section_re * twid_cos + section_im * twid_sin
    inner_im = section_im * twid_cos - section_re * twid_sin
    cos_two, sin_two = phase_table(second_idx, half_idx, FB)
    freq_re = jnp.einsum("rkb,bq->qkr", inner_re, cos_two, precision=best) + jnp.einsum(
        "rkb,bq->qkr", inner_im, sin_two, precision=best
    )
    freq_im = jnp.einsum("rkb,bq->qkr", inner_im, cos_two, precision=best) - jnp.einsum(
        "rkb,bq->qkr", inner_re, sin_two, precision=best
    )
    row_count = row_block.shape[0]
    return (freq_re.reshape(CH, row_count), freq_im.reshape(CH, row_count))


def correlate_kernel(
    spec_ref, gain_ref, delay_ref, vis_ref, power_ref, cur_re, cur_im, rot_re, rot_im, w_re, w_im
):
    step = pl.program_id(0)
    block = spec_ref.shape[1]
    spectra = spec_ref.shape[2]
    inputs = spec_ref.shape[3]
    beams = delay_ref.shape[0]

    @pl.when(step == 0)
    def _():
        chan_count = lax.axis_size("chan")
        first = (lax.axis_index("tm") * chan_count + lax.axis_index("chan")) * (
            block * pl.num_programs(0)
        )
        delays = delay_ref[...].T
        start = (delays * first % NFFT).astype(jnp.float32) * (2.0 * math.pi / NFFT)
        turn = delays.astype(jnp.float32) * (2.0 * math.pi / NFFT)
        norm = 1.0 / math.sqrt(inputs)
        cur_re[...] = jnp.cos(start) * norm
        cur_im[...] = -jnp.sin(start) * norm
        rot_re[...] = jnp.cos(turn)
        rot_im[...] = -jnp.sin(turn)

    rows = 16

    def advance(chunk, carry):
        at = pl.ds(pl.multiple_of(chunk * rows, rows), rows)
        c_re, c_im = cur_re[at, :], cur_im[at, :]
        r_re, r_im = rot_re[at, :], rot_im[at, :]
        for c in range(block):
            w_re[c, at, :] = c_re.astype(jnp.bfloat16)
            w_im[c, at, :] = c_im.astype(jnp.bfloat16)
            c_re, c_im = c_re * r_re - c_im * r_im, c_re * r_im + c_im * r_re
        cur_re[at, :] = c_re
        cur_im[at, :] = c_im
        return carry

    lax.fori_loop(0, inputs // rows, advance, 0)

    for c in range(block):
        a_re = spec_ref[0, c].astype(jnp.float32)
        a_im = spec_ref[1, c].astype(jnp.float32)
        g_re = gain_ref[0, c : c + 1, :]
        g_im = gain_ref[1, c : c + 1, :]
        cal_re = (g_re * a_re - g_im * a_im).astype(jnp.bfloat16)
        cal_im = (g_re * a_im + g_im * a_re).astype(jnp.bfloat16)
        stacked = jnp.concatenate([cal_re, cal_im], axis=0)
        flipped = jnp.concatenate([cal_im, -cal_re], axis=0)
        over_time = (((0,), (0,)), ((), ()))
        for part, left in enumerate((stacked, flipped)):
            vis = lax.dot_general(left, stacked, over_time, preferred_element_type=jnp.float32)
            vis_ref[part, c] = (vis * (1.0 / spectra)).astype(jnp.bfloat16)
        by_re = jnp.dot(stacked, w_re[c], preferred_element_type=jnp.float32)
        by_im = jnp.dot(stacked, w_im[c], preferred_element_type=jnp.float32)
        beam_re = by_re[:spectra] - by_im[spectra:]
        beam_im = by_re[spectra:] + by_im[:spectra]
        power_ref[c] = (beam_re * beam_re + beam_im * beam_im).astype(jnp.bfloat16)


def correlate(spectra, beam_delays, cal_gains):
    _, chan_local, spectra_total, inputs = spectra.shape
    beams = beam_delays.shape[0]
    block = math.gcd(chan_local, 8)
    table = pltpu.VMEM((inputs, beams), jnp.float32)
    return pl.pallas_call(
        correlate_kernel,
        grid=(chan_local // block,),
        in_specs=[
            pl.BlockSpec((2, block, spectra_total, inputs), lambda g: (0, g, 0, 0)),
            pl.BlockSpec((2, block, inputs), lambda g: (0, g, 0)),
            pl.BlockSpec((beams, inputs), lambda g: (0, 0)),
        ],
        out_specs=[
            pl.BlockSpec((2, block, inputs, inputs), lambda g: (0, g, 0, 0)),
            pl.BlockSpec((block, spectra_total, beams), lambda g: (g, 0, 0)),
        ],
        out_shape=[
            jax.ShapeDtypeStruct((2, chan_local, inputs, inputs), jnp.bfloat16),
            jax.ShapeDtypeStruct((chan_local, spectra_total, beams), jnp.bfloat16),
        ],
        scratch_shapes=[table] * 4 + [pltpu.VMEM((block, inputs, beams), jnp.bfloat16)] * 2,
        compiler_params=pltpu.CompilerParams(dimension_semantics=("arbitrary",)),
        name="correlate",
    )(spectra, cal_gains, beam_delays)


def shards(voltages, beam_delays, cal_gains):
    inp_dev = voltages.shape[0]
    spec_dev = voltages.shape[1] // NFFT
    tm_count = lax.axis_size("tm")
    chan_count = lax.axis_size("chan")
    spectra_total = spec_dev * tm_count
    raw_block = voltages.reshape(inp_dev, spec_dev, NFFT).transpose(1, 0, 2).astype(jnp.bfloat16)
    tail_block = shifted(raw_block[: TAPS - 1], "tm", -1)
    extended = jnp.concatenate([raw_block, tail_block], axis=0).astype(jnp.float32)
    coeffs = pfb_window()
    filtered = coeffs[0][None, None, :] * extended[0:spec_dev]
    for tap_index in range(1, TAPS):
        filtered = (
            filtered + coeffs[tap_index][None, None, :] * extended[tap_index : tap_index + spec_dev]
        )
    freq_re, freq_im = transform(filtered.reshape(spec_dev * inp_dev, FA, FB))
    packed = (jnp.stack([freq_re, freq_im]) * (1.0 / 64.0)).astype(jnp.bfloat16)
    packed = packed.reshape(2, CH, spec_dev, inp_dev)
    chan_local = CH // (tm_count * chan_count)
    reordered = packed.reshape(2, tm_count, chan_count, chan_local, spec_dev, inp_dev)
    reordered = reordered.transpose(0, 2, 1, 3, 4, 5).reshape(2, CH, spec_dev, inp_dev)
    sectioned = lax.all_to_all(reordered, "chan", split_axis=1, concat_axis=3, tiled=True)
    turned = lax.all_to_all(sectioned, "tm", split_axis=1, concat_axis=2, tiled=True)
    return correlate(turned, beam_delays, cal_gains)


def solution(mesh):
    return jax.shard_map(
        shards,
        mesh=mesh,
        in_specs=(P(("grp", "chan"), "tm"), P(), P(None, ("grp", "tm", "chan"), None)),
        out_specs=(
            P(None, ("grp", "tm", "chan"), None, None),
            P(("grp", "tm", "chan"), None, None),
        ),
        check_vma=False,
    )
```

```python
import functools
import math

import jax
import jax.numpy as jnp
import numpy as np
from jax import lax
from jax.experimental import pallas as pl
from jax.experimental.pallas import tpu as pltpu
from jax.sharding import PartitionSpec as P

TAPS = 4
FA = 64
FB = 64
NFFT = 4096
CH = 2048


def shifted(block, axis, distance):
    devices = range(lax.axis_size(axis))
    route = [(i - distance, i) for i in devices if i - distance in devices]
    return lax.ppermute(block, axis, route)


def pfb_window():
    total_len = TAPS * NFFT
    sample_pos = jnp.arange(total_len, dtype=jnp.float32)
    centre = (sample_pos - total_len / 2 + 0.5) / NFFT
    taper_win = 0.5 - 0.5 * jnp.cos(2.0 * math.pi * (sample_pos + 0.5) / total_len)
    coeffs = jnp.sinc(centre) * taper_win
    coeffs = coeffs / jnp.sqrt(jnp.sum(coeffs * coeffs))
    return coeffs.reshape(TAPS, NFFT)


RADIX = 32
LANES = NFFT // RADIX


def real_dft(rows):
    size = len(rows)
    if size == 2:
        return [(rows[0] + rows[1], None), (rows[0] - rows[1], None)]
    even, odd = real_dft(rows[0::2]), real_dft(rows[1::2])
    bins = [None] * (size // 2 + 1)
    bins[0] = (even[0][0] + odd[0][0], None)
    bins[size // 2] = (even[0][0] - odd[0][0], None)
    for k in range(1, size // 4):
        cos, sin = math.cos(2 * math.pi * k / size), math.sin(2 * math.pi * k / size)
        o_re, o_im = odd[k]
        t_re = o_re * cos + o_im * sin
        t_im = o_im * cos - o_re * sin
        bins[k] = (even[k][0] + t_re, even[k][1] + t_im)
        bins[size // 2 - k] = (even[k][0] - t_re, t_im - even[k][1])
    bins[size // 4] = (even[size // 4][0], -odd[size // 4][0])
    return bins


def twiddles():
    angle = 2.0 * np.pi * np.outer(np.arange(RADIX // 2 + 1), np.arange(LANES)) / NFFT
    table = np.stack([np.cos(angle), np.sin(angle)], axis=1).astype(np.float32)
    return np.broadcast_to(table[:, :, None, :], table.shape[:2] + (8, LANES))


def second_stage(groups):
    half = LANES // 2
    q = np.arange(LANES)
    angle = 2.0 * np.pi * (np.outer(q, q) % LANES) / LANES
    cos, sin = np.cos(angle) / 64.0, np.sin(angle) / 64.0
    real = np.concatenate([cos, sin], axis=1)
    imag = np.concatenate([-sin, cos], axis=1)
    plain = np.stack([real[:half], imag[:half]])
    mirror = np.stack([real[::-1][:half], -imag[::-1][:half]])
    none = np.zeros_like(plain)

    def ordered(first, second):
        rows = np.stack([first, second]).reshape(2, 2, groups, half // groups, 2 * LANES)
        return rows.transpose(2, 0, 1, 3, 4).reshape(2 * LANES, 2 * LANES)

    full = np.stack([ordered(plain, mirror), ordered(plain, none), ordered(none, plain)])
    high = full.astype(jnp.bfloat16)
    low = (full - high.astype(np.float64)).astype(jnp.bfloat16)
    return np.stack([high, low], axis=1)


def channelize_kernel(volt_ref, halo_ref, window_ref, twiddle_ref, dft_ref, out_ref, late, inner):
    inputs = volt_ref.shape[0]
    spectra = volt_ref.shape[1] // NFFT
    late[...] = halo_ref[...].astype(jnp.float32)

    def filter_rows(group, carry):
        first = pl.multiple_of(group * 8, 8)
        at = pl.ds(first, 8)
        for s in range(spectra):
            pieces = []
            for a in range(RADIX):
                total = None
                for tap in range(TAPS):
                    block = s + tap
                    if block < spectra:
                        col = block * NFFT + a * LANES
                        sample = volt_ref[at, col : col + LANES].astype(jnp.float32)
                    else:
                        col = (block - spectra) * NFFT + a * LANES
                        sample = late[at, col : col + LANES]
                    term = window_ref[tap, :, a * LANES : (a + 1) * LANES] * sample
                    total = term if total is None else total + term
                pieces.append(total)
            to = pl.ds(pl.multiple_of(s * inputs + first, 8), 8)
            for k, (re, im) in enumerate(real_dft(pieces)):
                cos, sin = twiddle_ref[k, 0], twiddle_ref[k, 1]
                if im is None:
                    inner[k, to, :LANES] = re * cos
                    inner[k, to, LANES:] = -re * sin
                else:
                    inner[k, to, :LANES] = re * cos + im * sin
                    inner[k, to, LANES:] = im * cos - re * sin
        return carry

    lax.fori_loop(0, inputs // 8, filter_rows, 0)

    def product(which, bins):
        over = (((1,), (1,)), ((), ()))
        dot = functools.partial(
            lax.dot_general, dimension_numbers=over, preferred_element_type=jnp.float32
        )
        high = bins.astype(jnp.bfloat16)
        low = (bins - high.astype(jnp.float32)).astype(jnp.bfloat16)
        return dot(dft_ref[which, 0], high) + (
            dot(dft_ref[which, 1], high) + dot(dft_ref[which, 0], low)
        )

    out_ref[0] = (product(1, inner[0]) + product(2, inner[RADIX // 2])).astype(jnp.bfloat16)

    def transform_bin(k, carry):
        out_ref[k] = product(0, inner[k]).astype(jnp.bfloat16)
        return carry

    lax.fori_loop(1, RADIX // 2, transform_bin, 0)


def channelize(voltages, halo, groups, **options):
    inputs = voltages.shape[0]
    rows = inputs * (voltages.shape[1] // NFFT)
    window = jnp.broadcast_to(pfb_window()[:, None, :], (TAPS, 8, NFFT))
    return pl.pallas_call(
        channelize_kernel,
        out_shape=jax.ShapeDtypeStruct((RADIX // 2, 2 * LANES, rows), jnp.bfloat16),
        scratch_shapes=[
            pltpu.VMEM(halo.shape, jnp.float32),
            pltpu.VMEM((RADIX // 2 + 1, rows, 2 * LANES), jnp.float32),
        ],
        name="channelize",
        **options,
    )(voltages, halo, window, twiddles(), second_stage(groups))


def correlate_kernel(
    spec_ref, gain_ref, delay_ref, vis_ref, power_ref, cur_re, cur_im, rot_re, rot_im, w_re, w_im
):
    step = pl.program_id(0)
    block = spec_ref.shape[1]
    spectra = spec_ref.shape[2]
    inputs = spec_ref.shape[3]
    beams = delay_ref.shape[0]

    @pl.when(step == 0)
    def _():
        chan_count = lax.axis_size("chan")
        first = (lax.axis_index("tm") * chan_count + lax.axis_index("chan")) * (
            block * pl.num_programs(0)
        )
        delays = delay_ref[...].T
        start = (delays * first % NFFT).astype(jnp.float32) * (2.0 * math.pi / NFFT)
        turn = delays.astype(jnp.float32) * (2.0 * math.pi / NFFT)
        norm = 1.0 / math.sqrt(inputs)
        cur_re[...] = jnp.cos(start) * norm
        cur_im[...] = -jnp.sin(start) * norm
        rot_re[...] = jnp.cos(turn)
        rot_im[...] = -jnp.sin(turn)

    rows = 16

    def advance(chunk, carry):
        at = pl.ds(pl.multiple_of(chunk * rows, rows), rows)
        c_re, c_im = cur_re[at, :], cur_im[at, :]
        r_re, r_im = rot_re[at, :], rot_im[at, :]
        for c in range(block):
            w_re[c, at, :] = c_re.astype(jnp.bfloat16)
            w_im[c, at, :] = c_im.astype(jnp.bfloat16)
            c_re, c_im = c_re * r_re - c_im * r_im, c_re * r_im + c_im * r_re
        cur_re[at, :] = c_re
        cur_im[at, :] = c_im
        return carry

    lax.fori_loop(0, inputs // rows, advance, 0)

    for c in range(block):
        a_re = spec_ref[0, c].astype(jnp.float32)
        a_im = spec_ref[1, c].astype(jnp.float32)
        g_re = gain_ref[0, c : c + 1, :]
        g_im = gain_ref[1, c : c + 1, :]
        cal_re = (g_re * a_re - g_im * a_im).astype(jnp.bfloat16)
        cal_im = (g_re * a_im + g_im * a_re).astype(jnp.bfloat16)
        stacked = jnp.concatenate([cal_re, cal_im], axis=0)
        flipped = jnp.concatenate([cal_im, -cal_re], axis=0)
        over_time = (((0,), (0,)), ((), ()))
        for part, left in enumerate((stacked, flipped)):
            vis = lax.dot_general(left, stacked, over_time, preferred_element_type=jnp.float32)
            vis_ref[part, c] = (vis * (1.0 / spectra)).astype(jnp.bfloat16)
        by_re = jnp.dot(stacked, w_re[c], preferred_element_type=jnp.float32)
        by_im = jnp.dot(stacked, w_im[c], preferred_element_type=jnp.float32)
        beam_re = by_re[:spectra] - by_im[spectra:]
        beam_im = by_re[spectra:] + by_im[:spectra]
        power_ref[c] = (beam_re * beam_re + beam_im * beam_im).astype(jnp.bfloat16)


def correlate(spectra, beam_delays, cal_gains):
    _, chan_local, spectra_total, inputs = spectra.shape
    beams = beam_delays.shape[0]
    block = math.gcd(chan_local, 8)
    table = pltpu.VMEM((inputs, beams), jnp.float32)
    return pl.pallas_call(
        correlate_kernel,
        grid=(chan_local // block,),
        in_specs=[
            pl.BlockSpec((2, block, spectra_total, inputs), lambda g: (0, g, 0, 0)),
            pl.BlockSpec((2, block, inputs), lambda g: (0, g, 0)),
            pl.BlockSpec((beams, inputs), lambda g: (0, 0)),
        ],
        out_specs=[
            pl.BlockSpec((2, block, inputs, inputs), lambda g: (0, g, 0, 0)),
            pl.BlockSpec((block, spectra_total, beams), lambda g: (g, 0, 0)),
        ],
        out_shape=[
            jax.ShapeDtypeStruct((2, chan_local, inputs, inputs), jnp.bfloat16),
            jax.ShapeDtypeStruct((chan_local, spectra_total, beams), jnp.bfloat16),
        ],
        scratch_shapes=[table] * 4 + [pltpu.VMEM((block, inputs, beams), jnp.bfloat16)] * 2,
        compiler_params=pltpu.CompilerParams(dimension_semantics=("arbitrary",)),
        name="correlate",
    )(spectra, cal_gains, beam_delays)


def shards(voltages, beam_delays, cal_gains):
    inp_dev = voltages.shape[0]
    spec_dev = voltages.shape[1] // NFFT
    tm_count = lax.axis_size("tm")
    chan_count = lax.axis_size("chan")
    spectra_total = spec_dev * tm_count
    halo = shifted(voltages[:, : (TAPS - 1) * NFFT].astype(jnp.bfloat16), "tm", -1)
    half = LANES // 2
    bins = channelize(voltages, halo, half).reshape(RADIX // 2, half, 2, 2, spec_dev, inp_dev)
    plain, mirror = bins[:, :, 0], bins[:, :, 1]
    bins = jnp.concatenate([plain, mirror[:1], mirror[:0:-1]], axis=0)
    packed = bins.transpose(2, 1, 0, 3, 4).reshape(2, CH, spec_dev, inp_dev)
    chan_local = CH // (tm_count * chan_count)
    reordered = packed.reshape(2, tm_count, chan_count, chan_local, spec_dev, inp_dev)
    reordered = reordered.transpose(0, 2, 1, 3, 4, 5).reshape(2, CH, spec_dev, inp_dev)
    sectioned = lax.all_to_all(reordered, "chan", split_axis=1, concat_axis=3, tiled=True)
    turned = lax.all_to_all(sectioned, "tm", split_axis=1, concat_axis=2, tiled=True)
    return correlate(turned, beam_delays, cal_gains)


def solution(mesh):
    return jax.shard_map(
        shards,
        mesh=mesh,
        in_specs=(P(("grp", "chan"), "tm"), P(), P(None, ("grp", "tm", "chan"), None)),
        out_specs=(
            P(None, ("grp", "tm", "chan"), None, None),
            P(("grp", "tm", "chan"), None, None),
        ),
        check_vma=False,
    )
```

```python
import functools
import math

import jax
import jax.numpy as jnp
import numpy as np
from jax import lax
from jax.experimental import pallas as pl
from jax.experimental.pallas import tpu as pltpu
from jax.sharding import PartitionSpec as P

TAPS = 4
FA = 64
FB = 64
NFFT = 4096
CH = 2048


def shifted(block, axis, distance):
    devices = range(lax.axis_size(axis))
    route = [(i - distance, i) for i in devices if i - distance in devices]
    return lax.ppermute(block, axis, route)


def pfb_window():
    total_len = TAPS * NFFT
    sample_pos = jnp.arange(total_len, dtype=jnp.float32)
    centre = (sample_pos - total_len / 2 + 0.5) / NFFT
    taper_win = 0.5 - 0.5 * jnp.cos(2.0 * math.pi * (sample_pos + 0.5) / total_len)
    coeffs = jnp.sinc(centre) * taper_win
    coeffs = coeffs / jnp.sqrt(jnp.sum(coeffs * coeffs))
    return coeffs.reshape(TAPS, NFFT)


RADIX = 32
LANES = NFFT // RADIX


def real_dft(rows):
    size = len(rows)
    if size == 2:
        return [(rows[0] + rows[1], None), (rows[0] - rows[1], None)]
    even, odd = real_dft(rows[0::2]), real_dft(rows[1::2])
    bins = [None] * (size // 2 + 1)
    bins[0] = (even[0][0] + odd[0][0], None)
    bins[size // 2] = (even[0][0] - odd[0][0], None)
    for k in range(1, size // 4):
        cos, sin = math.cos(2 * math.pi * k / size), math.sin(2 * math.pi * k / size)
        o_re, o_im = odd[k]
        t_re = o_re * cos + o_im * sin
        t_im = o_im * cos - o_re * sin
        bins[k] = (even[k][0] + t_re, even[k][1] + t_im)
        bins[size // 2 - k] = (even[k][0] - t_re, t_im - even[k][1])
    bins[size // 4] = (even[size // 4][0], -odd[size // 4][0])
    return bins


def twiddles():
    angle = 2.0 * np.pi * np.outer(np.arange(RADIX // 2 + 1), np.arange(LANES)) / NFFT
    table = np.stack([np.cos(angle), np.sin(angle)], axis=1).astype(np.float32)
    return np.broadcast_to(table[:, :, None, :], table.shape[:2] + (8, LANES))


def second_stage(groups):
    half = LANES // 2
    q = np.arange(LANES)
    angle = 2.0 * np.pi * (np.outer(q, q) % LANES) / LANES
    cos, sin = np.cos(angle) / 64.0, np.sin(angle) / 64.0
    real = np.concatenate([cos, sin], axis=1)
    imag = np.concatenate([-sin, cos], axis=1)
    plain = np.stack([real[:half], imag[:half]])
    mirror = np.stack([real[::-1][:half], -imag[::-1][:half]])
    none = np.zeros_like(plain)

    def ordered(first, second):
        rows = np.stack([first, second]).reshape(2, 2, groups, half // groups, 2 * LANES)
        return rows.transpose(2, 0, 1, 3, 4).reshape(2 * LANES, 2 * LANES)

    full = np.stack([ordered(plain, mirror), ordered(plain, none), ordered(none, plain)])
    high = full.astype(jnp.bfloat16)
    low = (full - high.astype(np.float64)).astype(jnp.bfloat16)
    return np.stack([high, low], axis=1)


def channelize_kernel(volt_ref, halo_ref, window_ref, twiddle_ref, dft_ref, out_ref, late, inner):
    inputs = volt_ref.shape[0]
    spectra = volt_ref.shape[1] // NFFT
    late[...] = halo_ref[...].astype(jnp.float32)

    def filter_rows(group, carry):
        first = pl.multiple_of(group * 8, 8)
        at = pl.ds(first, 8)
        for s in range(spectra):
            pieces = []
            for a in range(RADIX):
                total = None
                for tap in range(TAPS):
                    block = s + tap
                    if block < spectra:
                        col = block * NFFT + a * LANES
                        sample = volt_ref[at, col : col + LANES].astype(jnp.float32)
                    else:
                        col = (block - spectra) * NFFT + a * LANES
                        sample = late[at, col : col + LANES]
                    term = window_ref[tap, :, a * LANES : (a + 1) * LANES] * sample
                    total = term if total is None else total + term
                pieces.append(total)
            to = pl.ds(pl.multiple_of(s * inputs + first, 8), 8)
            for k, (re, im) in enumerate(real_dft(pieces)):
                cos, sin = twiddle_ref[k, 0], twiddle_ref[k, 1]
                if im is None:
                    inner[k, to, :LANES] = re * cos
                    inner[k, to, LANES:] = -re * sin
                else:
                    inner[k, to, :LANES] = re * cos + im * sin
                    inner[k, to, LANES:] = im * cos - re * sin
        return carry

    lax.fori_loop(0, inputs // 8, filter_rows, 0)

    def product(which, bins):
        over = (((1,), (1,)), ((), ()))
        dot = functools.partial(
            lax.dot_general, dimension_numbers=over, preferred_element_type=jnp.float32
        )
        high = bins.astype(jnp.bfloat16)
        low = (bins - high.astype(jnp.float32)).astype(jnp.bfloat16)
        return dot(dft_ref[which, 0], high) + (
            dot(dft_ref[which, 1], high) + dot(dft_ref[which, 0], low)
        )

    def put(k, value):
        groups, _, size, lanes = out_ref.shape
        out_ref[:, k] = value.astype(jnp.bfloat16).reshape(groups, size, lanes)

    put(0, product(1, inner[0]) + product(2, inner[RADIX // 2]))

    def transform_bin(k, carry):
        put(k, product(0, inner[k]))
        return carry

    lax.fori_loop(1, RADIX // 2, transform_bin, 0)


def channelize(voltages, halo, groups):
    inputs = voltages.shape[0]
    rows = inputs * (voltages.shape[1] // NFFT)
    window = jnp.broadcast_to(pfb_window()[:, None, :], (TAPS, 8, NFFT))
    return pl.pallas_call(
        channelize_kernel,
        out_shape=jax.ShapeDtypeStruct(
            (groups, RADIX // 2, 2 * LANES // groups, rows), jnp.bfloat16
        ),
        scratch_shapes=[
            pltpu.VMEM(halo.shape, jnp.float32),
            pltpu.VMEM((RADIX // 2 + 1, rows, 2 * LANES), jnp.float32),
        ],
        name="channelize",
    )(voltages, halo, window, twiddles(), second_stage(groups))


def exchange_kernel(out_ref, in_ref, send_sems, recv_sems, own_sem):
    tm_count, chan_count = lax.axis_size("tm"), lax.axis_size("chan")
    tm, chan = lax.axis_index("tm"), lax.axis_index("chan")
    slot = chan * tm_count + tm
    peers = []
    for tm_step in range(tm_count):
        for chan_step in range(chan_count):
            peer_tm = lax.rem(tm + tm_step, tm_count)
            peer_chan = lax.rem(chan + chan_step, chan_count)
            if tm_step or chan_step:
                peers.append((peer_tm, peer_chan))
    barrier = pltpu.get_barrier_semaphore()
    for peer_tm, peer_chan in peers:
        pl.semaphore_signal(
            barrier,
            inc=1,
            device_id={"tm": peer_tm, "chan": peer_chan},
            device_id_type=pl.DeviceIdType.MESH,
        )
    pl.semaphore_wait(barrier, len(peers))
    copies = []
    for index, (peer_tm, peer_chan) in enumerate(peers):
        copy = pltpu.make_async_remote_copy(
            src_ref=out_ref.at[peer_tm * chan_count + peer_chan],
            dst_ref=in_ref.at[slot],
            send_sem=send_sems.at[index],
            recv_sem=recv_sems.at[index],
            device_id={"tm": peer_tm, "chan": peer_chan},
            device_id_type=pl.DeviceIdType.MESH,
        )
        copy.start()
        copies.append(copy)
    own = pltpu.make_async_copy(out_ref.at[tm * chan_count + chan], in_ref.at[slot], own_sem)
    own.start()
    own.wait()
    for copy in copies:
        copy.wait()


def exchange(bins):
    return pl.pallas_call(
        exchange_kernel,
        in_specs=[pl.BlockSpec(memory_space=pl.ANY)],
        out_specs=pl.BlockSpec(memory_space=pl.ANY),
        out_shape=jax.ShapeDtypeStruct(bins.shape, bins.dtype),
        scratch_shapes=[
            pltpu.SemaphoreType.DMA((bins.shape[0] - 1,)),
            pltpu.SemaphoreType.DMA((bins.shape[0] - 1,)),
            pltpu.SemaphoreType.DMA,
        ],
        compiler_params=pltpu.CompilerParams(collective_id=0, has_side_effects=True),
        name="exchange",
    )(bins)


def correlate_bins_kernel(
    bins_ref, gain_ref, delay_ref, vis_ref, power_ref,
    cur_re, cur_im, rot_re, rot_im, far_re, far_im, w_re, w_im, rows_buf, power_buf,
):
    k1 = pl.program_id(0)
    tm_count, chan_count = lax.axis_size("tm"), lax.axis_size("chan")
    sources, _, size, lanes = bins_ref.shape
    block = vis_ref.shape[1]
    inputs = vis_ref.shape[4]
    own_inputs = inputs // chan_count
    spec_dev = lanes // own_inputs
    spectra = spec_dev * tm_count

    @pl.when(k1 == 0)
    def _():
        first = (lax.axis_index("tm") * chan_count + lax.axis_index("chan")) * (block * RADIX)
        delays = delay_ref[...].T
        norm = 1.0 / math.sqrt(inputs)

        def phase(steps):
            return (delays * steps % NFFT).astype(jnp.float32) * (2.0 * math.pi / NFFT)

        cur_re[...] = jnp.cos(phase(first)) * norm
        cur_im[...] = -jnp.sin(phase(first)) * norm
        rot_re[...] = jnp.cos(phase(1))
        rot_im[...] = -jnp.sin(phase(1))
        far_re[...] = jnp.cos(phase(RADIX))
        far_im[...] = -jnp.sin(phase(RADIX))

    rows = 16

    def advance(chunk, carry):
        at = pl.ds(pl.multiple_of(chunk * rows, rows), rows)
        c_re, c_im = cur_re[at, :], cur_im[at, :]
        r_re, r_im = rot_re[at, :], rot_im[at, :]
        cur_re[at, :] = c_re * r_re - c_im * r_im
        cur_im[at, :] = c_re * r_im + c_im * r_re
        r_re, r_im = far_re[at, :], far_im[at, :]
        for q in range(block):
            w_re[q, at, :] = c_re.astype(jnp.bfloat16)
            w_im[q, at, :] = c_im.astype(jnp.bfloat16)
            if q + 1 < block:
                c_re, c_im = c_re * r_re - c_im * r_im, c_re * r_im + c_im * r_re
        return carry

    lax.fori_loop(0, inputs // rows, advance, 0)

    received = bins_ref[...].astype(jnp.float32).reshape(sources * size, lanes)
    for part in range(lanes // LANES):
        rows_buf[part] = received[:, part * LANES : (part + 1) * LANES]
    mirror = jnp.where(k1 >= RADIX // 2, size // 2, 0)

    def gathered(row):
        parts = []
        for chan in range(chan_count):
            at = pl.ds(chan * tm_count * size + mirror + row, tm_count, stride=size)
            pieces = [rows_buf[part, at, :] for part in range(lanes // LANES)]
            parts.append(jnp.concatenate(pieces, axis=1))
        return jnp.concatenate(
            [
                jnp.concatenate([p[:, s * own_inputs : (s + 1) * own_inputs] for p in parts], axis=1)
                for s in range(spec_dev)
            ],
            axis=0,
        )

    g_re_all, g_im_all = gain_ref[0, :, 0], gain_ref[1, :, 0]
    for q in range(block):
        a_re, a_im = gathered(q), gathered(block + q)
        g_re, g_im = g_re_all[q], g_im_all[q]
        cal_re = (g_re * a_re - g_im * a_im).astype(jnp.bfloat16)
        cal_im = (g_re * a_im + g_im * a_re).astype(jnp.bfloat16)
        stacked = jnp.concatenate([cal_re, cal_im], axis=0)
        flipped = jnp.concatenate([cal_im, -cal_re], axis=0)
        over_time = (((0,), (0,)), ((), ()))
        for part, left in enumerate((stacked, flipped)):
            vis = lax.dot_general(left, stacked, over_time, preferred_element_type=jnp.float32)
            vis_ref[part, q, 0] = (vis * (1.0 / spectra)).astype(jnp.bfloat16)
        by_re = jnp.dot(stacked, w_re[q], preferred_element_type=jnp.float32)
        by_im = jnp.dot(stacked, w_im[q], preferred_element_type=jnp.float32)
        beam_re = by_re[:spectra] - by_im[spectra:]
        beam_im = by_re[spectra:] + by_im[:spectra]
        power = beam_re * beam_re + beam_im * beam_im
        for part in range(power.shape[1] // LANES):
            cols = slice(part * LANES, (part + 1) * LANES)
            power_buf[q, part] = power[:, cols]
            in_order = [
                power_buf[q, part, pl.ds(t, spec_dev, stride=tm_count), :] for t in range(tm_count)
            ]
            power_ref[q, 0, :, cols] = jnp.concatenate(in_order, axis=0).astype(jnp.bfloat16)


def correlate_bins(bins, beam_delays, cal_gains):
    sources, half, size, lanes = bins.shape
    _, chan_local, inputs = cal_gains.shape
    beams = beam_delays.shape[0]
    block = chan_local // RADIX
    spectra = sources * lanes // inputs
    table = pltpu.VMEM((inputs, beams), jnp.float32)
    vis, power = pl.pallas_call(
        correlate_bins_kernel,
        grid=(RADIX,),
        in_specs=[
            pl.BlockSpec(
                (sources, 1, size, lanes),
                lambda k: (0, jnp.where(k > half, RADIX - k, lax.rem(k, half)), 0, 0),
            ),
            pl.BlockSpec((2, block, 1, 1, inputs), lambda k: (0, 0, k, 0, 0)),
            pl.BlockSpec((beams, inputs), lambda k: (0, 0)),
        ],
        out_specs=[
            pl.BlockSpec((2, block, 1, inputs, inputs), lambda k: (0, 0, k, 0, 0)),
            pl.BlockSpec((block, 1, spectra, beams), lambda k: (0, k, 0, 0)),
        ],
        out_shape=[
            jax.ShapeDtypeStruct((2, block, RADIX, inputs, inputs), jnp.bfloat16),
            jax.ShapeDtypeStruct((block, RADIX, spectra, beams), jnp.bfloat16),
        ],
        scratch_shapes=[table] * 6
        + [pltpu.VMEM((block, inputs, beams), jnp.bfloat16)] * 2
        + [
            pltpu.VMEM((lanes // LANES, sources * size, LANES), jnp.float32),
            pltpu.VMEM((block, beams // LANES, spectra, LANES), jnp.float32),
        ],
        compiler_params=pltpu.CompilerParams(dimension_semantics=("arbitrary",)),
        name="correlate",
    )(bins, cal_gains.reshape(2, block, RADIX, 1, inputs), beam_delays)
    return (
        vis.reshape(2, chan_local, inputs, inputs),
        power.reshape(chan_local, spectra, beams),
    )


def correlate_kernel(
    spec_ref, gain_ref, delay_ref, vis_ref, power_ref, cur_re, cur_im, rot_re, rot_im, w_re, w_im
):
    step = pl.program_id(0)
    block = spec_ref.shape[1]
    spectra = spec_ref.shape[2]
    inputs = spec_ref.shape[3]
    beams = delay_ref.shape[0]

    @pl.when(step == 0)
    def _():
        chan_count = lax.axis_size("chan")
        first = (lax.axis_index("tm") * chan_count + lax.axis_index("chan")) * (
            block * pl.num_programs(0)
        )
        delays = delay_ref[...].T
        start = (delays * first % NFFT).astype(jnp.float32) * (2.0 * math.pi / NFFT)
        turn = delays.astype(jnp.float32) * (2.0 * math.pi / NFFT)
        norm = 1.0 / math.sqrt(inputs)
        cur_re[...] = jnp.cos(start) * norm
        cur_im[...] = -jnp.sin(start) * norm
        rot_re[...] = jnp.cos(turn)
        rot_im[...] = -jnp.sin(turn)

    rows = 16

    def advance(chunk, carry):
        at = pl.ds(pl.multiple_of(chunk * rows, rows), rows)
        c_re, c_im = cur_re[at, :], cur_im[at, :]
        r_re, r_im = rot_re[at, :], rot_im[at, :]
        for c in range(block):
            w_re[c, at, :] = c_re.astype(jnp.bfloat16)
            w_im[c, at, :] = c_im.astype(jnp.bfloat16)
            c_re, c_im = c_re * r_re - c_im * r_im, c_re * r_im + c_im * r_re
        cur_re[at, :] = c_re
        cur_im[at, :] = c_im
        return carry

    lax.fori_loop(0, inputs // rows, advance, 0)

    for c in range(block):
        a_re = spec_ref[0, c].astype(jnp.float32)
        a_im = spec_ref[1, c].astype(jnp.float32)
        g_re = gain_ref[0, c : c + 1, :]
        g_im = gain_ref[1, c : c + 1, :]
        cal_re = (g_re * a_re - g_im * a_im).astype(jnp.bfloat16)
        cal_im = (g_re * a_im + g_im * a_re).astype(jnp.bfloat16)
        stacked = jnp.concatenate([cal_re, cal_im], axis=0)
        flipped = jnp.concatenate([cal_im, -cal_re], axis=0)
        over_time = (((0,), (0,)), ((), ()))
        for part, left in enumerate((stacked, flipped)):
            vis = lax.dot_general(left, stacked, over_time, preferred_element_type=jnp.float32)
            vis_ref[part, c] = (vis * (1.0 / spectra)).astype(jnp.bfloat16)
        by_re = jnp.dot(stacked, w_re[c], preferred_element_type=jnp.float32)
        by_im = jnp.dot(stacked, w_im[c], preferred_element_type=jnp.float32)
        beam_re = by_re[:spectra] - by_im[spectra:]
        beam_im = by_re[spectra:] + by_im[:spectra]
        power_ref[c] = (beam_re * beam_re + beam_im * beam_im).astype(jnp.bfloat16)


def correlate(spectra, beam_delays, cal_gains):
    _, chan_local, spectra_total, inputs = spectra.shape
    beams = beam_delays.shape[0]
    block = math.gcd(chan_local, 8)
    table = pltpu.VMEM((inputs, beams), jnp.float32)
    return pl.pallas_call(
        correlate_kernel,
        grid=(chan_local // block,),
        in_specs=[
            pl.BlockSpec((2, block, spectra_total, inputs), lambda g: (0, g, 0, 0)),
            pl.BlockSpec((2, block, inputs), lambda g: (0, g, 0)),
            pl.BlockSpec((beams, inputs), lambda g: (0, 0)),
        ],
        out_specs=[
            pl.BlockSpec((2, block, inputs, inputs), lambda g: (0, g, 0, 0)),
            pl.BlockSpec((block, spectra_total, beams), lambda g: (g, 0, 0)),
        ],
        out_shape=[
            jax.ShapeDtypeStruct((2, chan_local, inputs, inputs), jnp.bfloat16),
            jax.ShapeDtypeStruct((chan_local, spectra_total, beams), jnp.bfloat16),
        ],
        scratch_shapes=[table] * 4 + [pltpu.VMEM((block, inputs, beams), jnp.bfloat16)] * 2,
        compiler_params=pltpu.CompilerParams(dimension_semantics=("arbitrary",)),
        name="correlate",
    )(spectra, cal_gains, beam_delays)


def shards(voltages, beam_delays, cal_gains):
    inp_dev = voltages.shape[0]
    spec_dev = voltages.shape[1] // NFFT
    tm_count = lax.axis_size("tm")
    chan_count = lax.axis_size("chan")
    spectra_total = spec_dev * tm_count
    halo = shifted(voltages[:, : (TAPS - 1) * NFFT].astype(jnp.bfloat16), "tm", -1)
    devices = tm_count * chan_count
    if CH % (4 * RADIX * devices) == 0:
        bins = exchange(channelize(voltages, halo, devices))
        return correlate_bins(bins, beam_delays, cal_gains)
    half = LANES // 2
    bins = channelize(voltages, halo, half).reshape(RADIX // 2, half, 2, 2, spec_dev, inp_dev)
    plain, mirror = bins[:, :, 0], bins[:, :, 1]
    bins = jnp.concatenate([plain, mirror[:1], mirror[:0:-1]], axis=0)
    packed = bins.transpose(2, 1, 0, 3, 4).reshape(2, CH, spec_dev, inp_dev)
    chan_local = CH // (tm_count * chan_count)
    reordered = packed.reshape(2, tm_count, chan_count, chan_local, spec_dev, inp_dev)
    reordered = reordered.transpose(0, 2, 1, 3, 4, 5).reshape(2, CH, spec_dev, inp_dev)
    sectioned = lax.all_to_all(reordered, "chan", split_axis=1, concat_axis=3, tiled=True)
    turned = lax.all_to_all(sectioned, "tm", split_axis=1, concat_axis=2, tiled=True)
    return correlate(turned, beam_delays, cal_gains)


def solution(mesh):
    return jax.shard_map(
        shards,
        mesh=mesh,
        in_specs=(P(("grp", "chan"), "tm"), P(), P(None, ("grp", "tm", "chan"), None)),
        out_specs=(
            P(None, ("grp", "tm", "chan"), None, None),
            P(("grp", "tm", "chan"), None, None),
        ),
        check_vma=False,
    )
```

```python
import functools
import math

import jax
import jax.numpy as jnp
import numpy as np
from jax import lax
from jax.experimental import pallas as pl
from jax.experimental.pallas import tpu as pltpu
from jax.sharding import PartitionSpec as P

TAPS = 4
FA = 64
FB = 64
NFFT = 4096
CH = 2048


def shifted(block, axis, distance):
    devices = range(lax.axis_size(axis))
    route = [(i - distance, i) for i in devices if i - distance in devices]
    return lax.ppermute(block, axis, route)


def pfb_window():
    total_len = TAPS * NFFT
    sample_pos = jnp.arange(total_len, dtype=jnp.float32)
    centre = (sample_pos - total_len / 2 + 0.5) / NFFT
    taper_win = 0.5 - 0.5 * jnp.cos(2.0 * math.pi * (sample_pos + 0.5) / total_len)
    coeffs = jnp.sinc(centre) * taper_win
    coeffs = coeffs / jnp.sqrt(jnp.sum(coeffs * coeffs))
    return coeffs.reshape(TAPS, NFFT)


RADIX = 32
LANES = NFFT // RADIX


def real_dft(rows):
    size = len(rows)
    if size == 2:
        return [(rows[0] + rows[1], None), (rows[0] - rows[1], None)]
    even, odd = real_dft(rows[0::2]), real_dft(rows[1::2])
    bins = [None] * (size // 2 + 1)
    bins[0] = (even[0][0] + odd[0][0], None)
    bins[size // 2] = (even[0][0] - odd[0][0], None)
    for k in range(1, size // 4):
        cos, sin = math.cos(2 * math.pi * k / size), math.sin(2 * math.pi * k / size)
        o_re, o_im = odd[k]
        t_re = o_re * cos + o_im * sin
        t_im = o_im * cos - o_re * sin
        bins[k] = (even[k][0] + t_re, even[k][1] + t_im)
        bins[size // 2 - k] = (even[k][0] - t_re, t_im - even[k][1])
    bins[size // 4] = (even[size // 4][0], -odd[size // 4][0])
    return bins


def twiddles():
    angle = 2.0 * np.pi * np.outer(np.arange(RADIX // 2 + 1), np.arange(LANES)) / NFFT
    table = np.stack([np.cos(angle), np.sin(angle)], axis=1).astype(np.float32)
    return np.broadcast_to(table[:, :, None, :], table.shape[:2] + (8, LANES))


def second_stage(groups):
    half = LANES // 2
    q = np.arange(LANES)
    angle = 2.0 * np.pi * (np.outer(q, q) % LANES) / LANES
    cos, sin = np.cos(angle) / 64.0, np.sin(angle) / 64.0
    real = np.concatenate([cos, sin], axis=1)
    imag = np.concatenate([-sin, cos], axis=1)
    plain = np.stack([real[:half], imag[:half]])
    mirror = np.stack([real[::-1][:half], -imag[::-1][:half]])
    none = np.zeros_like(plain)

    def ordered(first, second):
        rows = np.stack([first, second]).reshape(2, 2, groups, half // groups, 2 * LANES)
        return rows.transpose(2, 0, 1, 3, 4).reshape(2 * LANES, 2 * LANES)

    full = np.stack([ordered(plain, mirror), ordered(plain, none), ordered(none, plain)])
    high = full.astype(jnp.bfloat16)
    low = (full - high.astype(np.float64)).astype(jnp.bfloat16)
    return np.stack([high, low], axis=1)


def channelize_kernel(volt_ref, halo_ref, window_ref, twiddle_ref, dft_ref, out_ref, late, inner):
    inputs = volt_ref.shape[0]
    spectra = volt_ref.shape[1] // NFFT
    late[...] = halo_ref[...].astype(jnp.float32)

    def filter_rows(group, carry):
        first = pl.multiple_of(group * 8, 8)
        at = pl.ds(first, 8)
        for s in range(spectra):
            pieces = []
            for a in range(RADIX):
                total = None
                for tap in range(TAPS):
                    block = s + tap
                    if block < spectra:
                        col = block * NFFT + a * LANES
                        sample = volt_ref[at, col : col + LANES].astype(jnp.float32)
                    else:
                        col = (block - spectra) * NFFT + a * LANES
                        sample = late[at, col : col + LANES]
                    term = window_ref[tap, :, a * LANES : (a + 1) * LANES] * sample
                    total = term if total is None else total + term
                pieces.append(total)
            to = pl.ds(pl.multiple_of(s * inputs + first, 8), 8)
            for k, (re, im) in enumerate(real_dft(pieces)):
                cos, sin = twiddle_ref[k, 0], twiddle_ref[k, 1]
                if im is None:
                    inner[k, to, :LANES] = re * cos
                    inner[k, to, LANES:] = -re * sin
                else:
                    inner[k, to, :LANES] = re * cos + im * sin
                    inner[k, to, LANES:] = im * cos - re * sin
        return carry

    lax.fori_loop(0, inputs // 8, filter_rows, 0)

    def product(which, bins):
        over = (((1,), (1,)), ((), ()))
        dot = functools.partial(
            lax.dot_general, dimension_numbers=over, preferred_element_type=jnp.float32
        )
        high = bins.astype(jnp.bfloat16)
        low = (bins - high.astype(jnp.float32)).astype(jnp.bfloat16)
        return dot(dft_ref[which, 0], high) + (
            dot(dft_ref[which, 1], high) + dot(dft_ref[which, 0], low)
        )

    def put(k, value):
        groups, _, size, lanes = out_ref.shape
        out_ref[:, k] = value.astype(jnp.bfloat16).reshape(groups, size, lanes)

    put(0, product(1, inner[0]) + product(2, inner[RADIX // 2]))

    def transform_bin(k, carry):
        put(k, product(0, inner[k]))
        return carry

    lax.fori_loop(1, RADIX // 2, transform_bin, 0)


def channelize(voltages, halo, groups):
    inputs = voltages.shape[0]
    rows = inputs * (voltages.shape[1] // NFFT)
    window = jnp.broadcast_to(pfb_window()[:, None, :], (TAPS, 8, NFFT))
    return pl.pallas_call(
        channelize_kernel,
        out_shape=jax.ShapeDtypeStruct(
            (groups, RADIX // 2, 2 * LANES // groups, rows), jnp.bfloat16
        ),
        scratch_shapes=[
            pltpu.VMEM(halo.shape, jnp.float32),
            pltpu.VMEM((RADIX // 2 + 1, rows, 2 * LANES), jnp.float32),
        ],
        name="channelize",
    )(voltages, halo, window, twiddles(), second_stage(groups))


def exchange_kernel(out_ref, in_ref, send_sems, recv_sems, own_sem):
    tm_count, chan_count = lax.axis_size("tm"), lax.axis_size("chan")
    tm, chan = lax.axis_index("tm"), lax.axis_index("chan")
    slot = chan * tm_count + tm
    peers = []
    for tm_step in range(tm_count):
        for chan_step in range(chan_count):
            peer_tm = lax.rem(tm + tm_step, tm_count)
            peer_chan = lax.rem(chan + chan_step, chan_count)
            if tm_step or chan_step:
                peers.append((peer_tm, peer_chan))
    barrier = pltpu.get_barrier_semaphore()
    for peer_tm, peer_chan in peers:
        pl.semaphore_signal(
            barrier,
            inc=1,
            device_id={"tm": peer_tm, "chan": peer_chan},
            device_id_type=pl.DeviceIdType.MESH,
        )
    pl.semaphore_wait(barrier, len(peers))
    copies = []
    for index, (peer_tm, peer_chan) in enumerate(peers):
        copy = pltpu.make_async_remote_copy(
            src_ref=out_ref.at[peer_tm * chan_count + peer_chan],
            dst_ref=in_ref.at[slot],
            send_sem=send_sems.at[index],
            recv_sem=recv_sems.at[index],
            device_id={"tm": peer_tm, "chan": peer_chan},
            device_id_type=pl.DeviceIdType.MESH,
        )
        copy.start()
        copies.append(copy)
    own = pltpu.make_async_copy(out_ref.at[tm * chan_count + chan], in_ref.at[slot], own_sem)
    own.start()
    own.wait()
    for copy in copies:
        copy.wait()


def exchange(bins):
    return pl.pallas_call(
        exchange_kernel,
        in_specs=[pl.BlockSpec(memory_space=pl.ANY)],
        out_specs=pl.BlockSpec(memory_space=pl.ANY),
        out_shape=jax.ShapeDtypeStruct(bins.shape, bins.dtype),
        scratch_shapes=[
            pltpu.SemaphoreType.DMA((bins.shape[0] - 1,)),
            pltpu.SemaphoreType.DMA((bins.shape[0] - 1,)),
            pltpu.SemaphoreType.DMA,
        ],
        compiler_params=pltpu.CompilerParams(collective_id=0, has_side_effects=True),
        name="exchange",
    )(bins)


def weights_kernel(delay_ref, out_ref, cur_re, cur_im, rot_re, rot_im, far_re, far_im):
    k1 = pl.program_id(0)
    block = out_ref.shape[1]
    inputs = out_ref.shape[3]

    @pl.when(k1 == 0)
    def _():
        device = lax.axis_index("tm") * lax.axis_size("chan") + lax.axis_index("chan")
        first = device * (block * RADIX)
        delays = delay_ref[...].T
        norm = 1.0 / math.sqrt(inputs)

        def phase(steps):
            return (delays * steps % NFFT).astype(jnp.float32) * (2.0 * math.pi / NFFT)

        cur_re[...] = jnp.cos(phase(first)) * norm
        cur_im[...] = -jnp.sin(phase(first)) * norm
        rot_re[...] = jnp.cos(phase(1))
        rot_im[...] = -jnp.sin(phase(1))
        far_re[...] = jnp.cos(phase(RADIX))
        far_im[...] = -jnp.sin(phase(RADIX))

    rows = 16

    def advance(chunk, carry):
        at = pl.ds(pl.multiple_of(chunk * rows, rows), rows)
        c_re, c_im = cur_re[at, :], cur_im[at, :]
        r_re, r_im = rot_re[at, :], rot_im[at, :]
        cur_re[at, :] = c_re * r_re - c_im * r_im
        cur_im[at, :] = c_re * r_im + c_im * r_re
        r_re, r_im = far_re[at, :], far_im[at, :]
        for q in range(block):
            out_ref[0, q, 0, at, :] = c_re.astype(jnp.bfloat16)
            out_ref[0, q, 1, at, :] = c_im.astype(jnp.bfloat16)
            if q + 1 < block:
                c_re, c_im = c_re * r_re - c_im * r_im, c_re * r_im + c_im * r_re
        return carry

    lax.fori_loop(0, inputs // rows, advance, 0)


def beam_weights(beam_delays, block):
    beams, inputs = beam_delays.shape
    shape = (RADIX, block, 2, inputs, beams)
    return pl.pallas_call(
        weights_kernel,
        grid=(RADIX,),
        in_specs=[pl.BlockSpec((beams, inputs), lambda k: (0, 0))],
        out_specs=pl.BlockSpec((1,) + shape[1:], lambda k: (k, 0, 0, 0, 0)),
        out_shape=jax.ShapeDtypeStruct(shape, jnp.bfloat16),
        scratch_shapes=[pltpu.VMEM((inputs, beams), jnp.float32)] * 6,
        compiler_params=pltpu.CompilerParams(dimension_semantics=("arbitrary",)),
        cost_estimate=pl.CostEstimate(
            flops=12 * math.prod(shape), bytes_accessed=2 * math.prod(shape), transcendentals=0
        ),
        name="beam_weights",
    )(beam_delays)


def correlate_bins_kernel(
    bins_ref, gain_ref, weight_ref, vis_ref, power_ref, rows_buf, power_buf
):
    k1 = pl.program_id(0)
    tm_count, chan_count = lax.axis_size("tm"), lax.axis_size("chan")
    sources, _, size, lanes = bins_ref.shape
    block = vis_ref.shape[1]
    inputs = vis_ref.shape[4]
    own_inputs = inputs // chan_count
    spec_dev = lanes // own_inputs
    spectra = spec_dev * tm_count

    received = bins_ref[...].astype(jnp.float32).reshape(sources * size, lanes)
    for part in range(lanes // LANES):
        rows_buf[part] = received[:, part * LANES : (part + 1) * LANES]
    mirror = jnp.where(k1 >= RADIX // 2, size // 2, 0)

    def gathered(row):
        parts = []
        for chan in range(chan_count):
            at = pl.ds(chan * tm_count * size + mirror + row, tm_count, stride=size)
            pieces = [rows_buf[part, at, :] for part in range(lanes // LANES)]
            parts.append(jnp.concatenate(pieces, axis=1))
        return jnp.concatenate(
            [
                jnp.concatenate([p[:, s * own_inputs : (s + 1) * own_inputs] for p in parts], axis=1)
                for s in range(spec_dev)
            ],
            axis=0,
        )

    g_re_all, g_im_all = gain_ref[0, :, 0], gain_ref[1, :, 0]
    ready = []
    for q in range(block):
        a_re, a_im = gathered(q), gathered(block + q)
        g_re, g_im = g_re_all[q], g_im_all[q]
        cal_re = (g_re * a_re - g_im * a_im).astype(jnp.bfloat16)
        cal_im = (g_re * a_im + g_im * a_re).astype(jnp.bfloat16)
        stacked = jnp.concatenate([cal_re, cal_im], axis=0)
        flipped = jnp.concatenate([cal_im, -cal_re], axis=0)
        ready.append((stacked, flipped))
    over_time = (((0,), (0,)), ((), ()))
    for q, (stacked, flipped) in enumerate(ready):
        for part, left in enumerate((stacked, flipped)):
            vis = lax.dot_general(left, stacked, over_time, preferred_element_type=jnp.float32)
            vis_ref[part, q, 0] = (vis * (1.0 / spectra)).astype(jnp.bfloat16)
        by_re = jnp.dot(stacked, weight_ref[0, q, 0], preferred_element_type=jnp.float32)
        by_im = jnp.dot(stacked, weight_ref[0, q, 1], preferred_element_type=jnp.float32)
        beam_re = by_re[:spectra] - by_im[spectra:]
        beam_im = by_re[spectra:] + by_im[:spectra]
        power = beam_re * beam_re + beam_im * beam_im
        for part in range(power.shape[1] // LANES):
            cols = slice(part * LANES, (part + 1) * LANES)
            power_buf[q, part] = power[:, cols]
            in_order = [
                power_buf[q, part, pl.ds(t, spec_dev, stride=tm_count), :] for t in range(tm_count)
            ]
            power_ref[q, 0, :, cols] = jnp.concatenate(in_order, axis=0).astype(jnp.bfloat16)


def correlate_bins(bins, weights, cal_gains):
    sources, half, size, lanes = bins.shape
    _, chan_local, inputs = cal_gains.shape
    beams = weights.shape[4]
    block = chan_local // RADIX
    spectra = sources * lanes // inputs
    vis, power = pl.pallas_call(
        correlate_bins_kernel,
        grid=(RADIX,),
        in_specs=[
            pl.BlockSpec(
                (sources, 1, size, lanes),
                lambda k: (0, jnp.where(k > half, RADIX - k, lax.rem(k, half)), 0, 0),
            ),
            pl.BlockSpec((2, block, 1, 1, inputs), lambda k: (0, 0, k, 0, 0)),
            pl.BlockSpec((1, block, 2, inputs, beams), lambda k: (k, 0, 0, 0, 0)),
        ],
        out_specs=[
            pl.BlockSpec((2, block, 1, inputs, inputs), lambda k: (0, 0, k, 0, 0)),
            pl.BlockSpec((block, 1, spectra, beams), lambda k: (0, k, 0, 0)),
        ],
        out_shape=[
            jax.ShapeDtypeStruct((2, block, RADIX, inputs, inputs), jnp.bfloat16),
            jax.ShapeDtypeStruct((block, RADIX, spectra, beams), jnp.bfloat16),
        ],
        scratch_shapes=[
            pltpu.VMEM((lanes // LANES, sources * size, LANES), jnp.float32),
            pltpu.VMEM((block, beams // LANES, spectra, LANES), jnp.float32),
        ],
        compiler_params=pltpu.CompilerParams(dimension_semantics=("arbitrary",)),
        name="correlate",
    )(bins, cal_gains.reshape(2, block, RADIX, 1, inputs), weights)
    return (
        vis.reshape(2, chan_local, inputs, inputs),
        power.reshape(chan_local, spectra, beams),
    )


def correlate_kernel(
    spec_ref, gain_ref, delay_ref, vis_ref, power_ref, cur_re, cur_im, rot_re, rot_im, w_re, w_im
):
    step = pl.program_id(0)
    block = spec_ref.shape[1]
    spectra = spec_ref.shape[2]
    inputs = spec_ref.shape[3]
    beams = delay_ref.shape[0]

    @pl.when(step == 0)
    def _():
        chan_count = lax.axis_size("chan")
        first = (lax.axis_index("tm") * chan_count + lax.axis_index("chan")) * (
            block * pl.num_programs(0)
        )
        delays = delay_ref[...].T
        start = (delays * first % NFFT).astype(jnp.float32) * (2.0 * math.pi / NFFT)
        turn = delays.astype(jnp.float32) * (2.0 * math.pi / NFFT)
        norm = 1.0 / math.sqrt(inputs)
        cur_re[...] = jnp.cos(start) * norm
        cur_im[...] = -jnp.sin(start) * norm
        rot_re[...] = jnp.cos(turn)
        rot_im[...] = -jnp.sin(turn)

    rows = 16

    def advance(chunk, carry):
        at = pl.ds(pl.multiple_of(chunk * rows, rows), rows)
        c_re, c_im = cur_re[at, :], cur_im[at, :]
        r_re, r_im = rot_re[at, :], rot_im[at, :]
        for c in range(block):
            w_re[c, at, :] = c_re.astype(jnp.bfloat16)
            w_im[c, at, :] = c_im.astype(jnp.bfloat16)
            c_re, c_im = c_re * r_re - c_im * r_im, c_re * r_im + c_im * r_re
        cur_re[at, :] = c_re
        cur_im[at, :] = c_im
        return carry

    lax.fori_loop(0, inputs // rows, advance, 0)

    for c in range(block):
        a_re = spec_ref[0, c].astype(jnp.float32)
        a_im = spec_ref[1, c].astype(jnp.float32)
        g_re = gain_ref[0, c : c + 1, :]
        g_im = gain_ref[1, c : c + 1, :]
        cal_re = (g_re * a_re - g_im * a_im).astype(jnp.bfloat16)
        cal_im = (g_re * a_im + g_im * a_re).astype(jnp.bfloat16)
        stacked = jnp.concatenate([cal_re, cal_im], axis=0)
        flipped = jnp.concatenate([cal_im, -cal_re], axis=0)
        over_time = (((0,), (0,)), ((), ()))
        for part, left in enumerate((stacked, flipped)):
            vis = lax.dot_general(left, stacked, over_time, preferred_element_type=jnp.float32)
            vis_ref[part, c] = (vis * (1.0 / spectra)).astype(jnp.bfloat16)
        by_re = jnp.dot(stacked, w_re[c], preferred_element_type=jnp.float32)
        by_im = jnp.dot(stacked, w_im[c], preferred_element_type=jnp.float32)
        beam_re = by_re[:spectra] - by_im[spectra:]
        beam_im = by_re[spectra:] + by_im[:spectra]
        power_ref[c] = (beam_re * beam_re + beam_im * beam_im).astype(jnp.bfloat16)


def correlate(spectra, beam_delays, cal_gains):
    _, chan_local, spectra_total, inputs = spectra.shape
    beams = beam_delays.shape[0]
    block = math.gcd(chan_local, 8)
    table = pltpu.VMEM((inputs, beams), jnp.float32)
    return pl.pallas_call(
        correlate_kernel,
        grid=(chan_local // block,),
        in_specs=[
            pl.BlockSpec((2, block, spectra_total, inputs), lambda g: (0, g, 0, 0)),
            pl.BlockSpec((2, block, inputs), lambda g: (0, g, 0)),
            pl.BlockSpec((beams, inputs), lambda g: (0, 0)),
        ],
        out_specs=[
            pl.BlockSpec((2, block, inputs, inputs), lambda g: (0, g, 0, 0)),
            pl.BlockSpec((block, spectra_total, beams), lambda g: (g, 0, 0)),
        ],
        out_shape=[
            jax.ShapeDtypeStruct((2, chan_local, inputs, inputs), jnp.bfloat16),
            jax.ShapeDtypeStruct((chan_local, spectra_total, beams), jnp.bfloat16),
        ],
        scratch_shapes=[table] * 4 + [pltpu.VMEM((block, inputs, beams), jnp.bfloat16)] * 2,
        compiler_params=pltpu.CompilerParams(dimension_semantics=("arbitrary",)),
        name="correlate",
    )(spectra, cal_gains, beam_delays)


def shards(voltages, beam_delays, cal_gains):
    inp_dev = voltages.shape[0]
    spec_dev = voltages.shape[1] // NFFT
    tm_count = lax.axis_size("tm")
    chan_count = lax.axis_size("chan")
    spectra_total = spec_dev * tm_count
    halo = shifted(voltages[:, : (TAPS - 1) * NFFT].astype(jnp.bfloat16), "tm", -1)
    devices = tm_count * chan_count
    if CH % (4 * RADIX * devices) == 0:
        weights = beam_weights(beam_delays, CH // devices // RADIX)
        bins = exchange(channelize(voltages, halo, devices))
        return correlate_bins(bins, weights, cal_gains)
    half = LANES // 2
    bins = channelize(voltages, halo, half).reshape(RADIX // 2, half, 2, 2, spec_dev, inp_dev)
    plain, mirror = bins[:, :, 0], bins[:, :, 1]
    bins = jnp.concatenate([plain, mirror[:1], mirror[:0:-1]], axis=0)
    packed = bins.transpose(2, 1, 0, 3, 4).reshape(2, CH, spec_dev, inp_dev)
    chan_local = CH // (tm_count * chan_count)
    reordered = packed.reshape(2, tm_count, chan_count, chan_local, spec_dev, inp_dev)
    reordered = reordered.transpose(0, 2, 1, 3, 4, 5).reshape(2, CH, spec_dev, inp_dev)
    sectioned = lax.all_to_all(reordered, "chan", split_axis=1, concat_axis=3, tiled=True)
    turned = lax.all_to_all(sectioned, "tm", split_axis=1, concat_axis=2, tiled=True)
    return correlate(turned, beam_delays, cal_gains)


def solution(mesh):
    return jax.shard_map(
        shards,
        mesh=mesh,
        in_specs=(P(("grp", "chan"), "tm"), P(), P(None, ("grp", "tm", "chan"), None)),
        out_specs=(
            P(None, ("grp", "tm", "chan"), None, None),
            P(("grp", "tm", "chan"), None, None),
        ),
        check_vma=False,
    )
```

```python
import functools
import math

import jax
import jax.numpy as jnp
import numpy as np
from jax import lax
from jax.experimental import pallas as pl
from jax.experimental.pallas import tpu as pltpu
from jax.sharding import PartitionSpec as P

TAPS = 4
FA = 64
FB = 64
NFFT = 4096
CH = 2048


def shifted(block, axis, distance):
    devices = range(lax.axis_size(axis))
    route = [(i - distance, i) for i in devices if i - distance in devices]
    return lax.ppermute(block, axis, route)


def pfb_window():
    total_len = TAPS * NFFT
    sample_pos = jnp.arange(total_len, dtype=jnp.float32)
    centre = (sample_pos - total_len / 2 + 0.5) / NFFT
    taper_win = 0.5 - 0.5 * jnp.cos(2.0 * math.pi * (sample_pos + 0.5) / total_len)
    coeffs = jnp.sinc(centre) * taper_win
    coeffs = coeffs / jnp.sqrt(jnp.sum(coeffs * coeffs))
    return coeffs.reshape(TAPS, NFFT)


RADIX = 32
LANES = NFFT // RADIX


def real_dft(rows):
    size = len(rows)
    if size == 2:
        return [(rows[0] + rows[1], None), (rows[0] - rows[1], None)]
    even, odd = real_dft(rows[0::2]), real_dft(rows[1::2])
    bins = [None] * (size // 2 + 1)
    bins[0] = (even[0][0] + odd[0][0], None)
    bins[size // 2] = (even[0][0] - odd[0][0], None)
    for k in range(1, size // 4):
        cos, sin = math.cos(2 * math.pi * k / size), math.sin(2 * math.pi * k / size)
        o_re, o_im = odd[k]
        t_re = o_re * cos + o_im * sin
        t_im = o_im * cos - o_re * sin
        bins[k] = (even[k][0] + t_re, even[k][1] + t_im)
        bins[size // 2 - k] = (even[k][0] - t_re, t_im - even[k][1])
    bins[size // 4] = (even[size // 4][0], -odd[size // 4][0])
    return bins


def twiddles():
    angle = 2.0 * np.pi * np.outer(np.arange(RADIX // 2 + 1), np.arange(LANES)) / NFFT
    table = np.stack([np.cos(angle), np.sin(angle)], axis=1).astype(np.float32)
    return np.broadcast_to(table[:, :, None, :], table.shape[:2] + (8, LANES))


def second_stage(groups):
    half = LANES // 2
    q = np.arange(LANES)
    angle = 2.0 * np.pi * (np.outer(q, q) % LANES) / LANES
    cos, sin = np.cos(angle) / 64.0, np.sin(angle) / 64.0
    real = np.concatenate([cos, sin], axis=1)
    imag = np.concatenate([-sin, cos], axis=1)
    plain = np.stack([real[:half], imag[:half]])
    mirror = np.stack([real[::-1][:half], -imag[::-1][:half]])
    none = np.zeros_like(plain)

    def ordered(first, second):
        rows = np.stack([first, second]).reshape(2, 2, groups, half // groups, 2 * LANES)
        return rows.transpose(2, 0, 1, 3, 4).reshape(2 * LANES, 2 * LANES)

    full = np.stack([ordered(plain, mirror), ordered(plain, none), ordered(none, plain)])
    high = full.astype(jnp.bfloat16)
    low = (full - high.astype(np.float64)).astype(jnp.bfloat16)
    return np.stack([high, low], axis=1)


def channelize_kernel(volt_ref, halo_ref, window_ref, twiddle_ref, dft_ref, out_ref, late, inner):
    inputs = volt_ref.shape[0]
    spectra = volt_ref.shape[1] // NFFT
    late[...] = halo_ref[...].astype(jnp.float32)

    def filter_rows(group, carry):
        first = pl.multiple_of(group * 8, 8)
        at = pl.ds(first, 8)
        for s in range(spectra):
            pieces = []
            for a in range(RADIX):
                total = None
                for tap in range(TAPS):
                    block = s + tap
                    if block < spectra:
                        col = block * NFFT + a * LANES
                        sample = volt_ref[at, col : col + LANES].astype(jnp.float32)
                    else:
                        col = (block - spectra) * NFFT + a * LANES
                        sample = late[at, col : col + LANES]
                    term = window_ref[tap, :, a * LANES : (a + 1) * LANES] * sample
                    total = term if total is None else total + term
                pieces.append(total)
            to = pl.ds(pl.multiple_of(s * inputs + first, 8), 8)
            for k, (re, im) in enumerate(real_dft(pieces)):
                cos, sin = twiddle_ref[k, 0], twiddle_ref[k, 1]
                if im is None:
                    inner[k, to, :LANES] = re * cos
                    inner[k, to, LANES:] = -re * sin
                else:
                    inner[k, to, :LANES] = re * cos + im * sin
                    inner[k, to, LANES:] = im * cos - re * sin
        return carry

    lax.fori_loop(0, inputs // 8, filter_rows, 0)

    def product(which, bins):
        over = (((1,), (1,)), ((), ()))
        dot = functools.partial(
            lax.dot_general, dimension_numbers=over, preferred_element_type=jnp.float32
        )
        high = bins.astype(jnp.bfloat16)
        low = (bins - high.astype(jnp.float32)).astype(jnp.bfloat16)
        return dot(dft_ref[which, 0], high) + (
            dot(dft_ref[which, 1], high) + dot(dft_ref[which, 0], low)
        )

    def put(k, value):
        groups, _, size, lanes = out_ref.shape
        out_ref[:, k] = value.astype(jnp.bfloat16).reshape(groups, size, lanes)

    put(0, product(1, inner[0]) + product(2, inner[RADIX // 2]))

    def transform_bin(k, carry):
        put(k, product(0, inner[k]))
        return carry

    lax.fori_loop(1, RADIX // 2, transform_bin, 0)


def channelize(voltages, halo, groups):
    inputs = voltages.shape[0]
    rows = inputs * (voltages.shape[1] // NFFT)
    window = jnp.broadcast_to(pfb_window()[:, None, :], (TAPS, 8, NFFT))
    return pl.pallas_call(
        channelize_kernel,
        out_shape=jax.ShapeDtypeStruct(
            (groups, RADIX // 2, 2 * LANES // groups, rows), jnp.bfloat16
        ),
        scratch_shapes=[
            pltpu.VMEM(halo.shape, jnp.float32),
            pltpu.VMEM((RADIX // 2 + 1, rows, 2 * LANES), jnp.float32),
        ],
        name="channelize",
    )(voltages, halo, window, twiddles(), second_stage(groups))


def exchange_kernel(out_ref, in_ref, send_sems, recv_sems, own_sem):
    tm_count, chan_count = lax.axis_size("tm"), lax.axis_size("chan")
    tm, chan = lax.axis_index("tm"), lax.axis_index("chan")
    slot = chan * tm_count + tm
    peers = []
    for tm_step in range(tm_count):
        for chan_step in range(chan_count):
            peer_tm = lax.rem(tm + tm_step, tm_count)
            peer_chan = lax.rem(chan + chan_step, chan_count)
            if tm_step or chan_step:
                peers.append((peer_tm, peer_chan))
    barrier = pltpu.get_barrier_semaphore()
    for peer_tm, peer_chan in peers:
        pl.semaphore_signal(
            barrier,
            inc=1,
            device_id={"tm": peer_tm, "chan": peer_chan},
            device_id_type=pl.DeviceIdType.MESH,
        )
    pl.semaphore_wait(barrier, len(peers))
    copies = []
    for index, (peer_tm, peer_chan) in enumerate(peers):
        copy = pltpu.make_async_remote_copy(
            src_ref=out_ref.at[peer_tm * chan_count + peer_chan],
            dst_ref=in_ref.at[slot],
            send_sem=send_sems.at[index],
            recv_sem=recv_sems.at[index],
            device_id={"tm": peer_tm, "chan": peer_chan},
            device_id_type=pl.DeviceIdType.MESH,
        )
        copy.start()
        copies.append(copy)
    own = pltpu.make_async_copy(out_ref.at[tm * chan_count + chan], in_ref.at[slot], own_sem)
    own.start()
    own.wait()
    for copy in copies:
        copy.wait()


def exchange(bins):
    return pl.pallas_call(
        exchange_kernel,
        in_specs=[pl.BlockSpec(memory_space=pl.ANY)],
        out_specs=pl.BlockSpec(memory_space=pl.ANY),
        out_shape=jax.ShapeDtypeStruct(bins.shape, bins.dtype),
        scratch_shapes=[
            pltpu.SemaphoreType.DMA((bins.shape[0] - 1,)),
            pltpu.SemaphoreType.DMA((bins.shape[0] - 1,)),
            pltpu.SemaphoreType.DMA,
        ],
        compiler_params=pltpu.CompilerParams(collective_id=0, has_side_effects=True),
        name="exchange",
    )(bins)


def correlate_bins_kernel(
    bins_ref, gain_ref, delay_ref, vis_ref, power_ref,
    cur_re, cur_im, rot_re, rot_im, far_re, far_im, w_re, w_im, rows_buf, power_buf,
):
    k1 = pl.program_id(0)
    tm_count, chan_count = lax.axis_size("tm"), lax.axis_size("chan")
    sources, _, size, lanes = bins_ref.shape
    block = vis_ref.shape[1]
    inputs = vis_ref.shape[4]
    own_inputs = inputs // chan_count
    spec_dev = lanes // own_inputs
    spectra = spec_dev * tm_count

    @pl.when(k1 == 0)
    def _():
        first = (lax.axis_index("tm") * chan_count + lax.axis_index("chan")) * (block * RADIX)
        delays = delay_ref[...].T
        norm = 1.0 / math.sqrt(inputs)

        def phase(steps):
            return (delays * steps % NFFT).astype(jnp.float32) * (2.0 * math.pi / NFFT)

        cur_re[...] = jnp.cos(phase(first)) * norm
        cur_im[...] = -jnp.sin(phase(first)) * norm
        rot_re[...] = jnp.cos(phase(1))
        rot_im[...] = -jnp.sin(phase(1))
        far_re[...] = jnp.cos(phase(RADIX))
        far_im[...] = -jnp.sin(phase(RADIX))

    rows = 16

    def advance(chunk, carry):
        at = pl.ds(pl.multiple_of(chunk * rows, rows), rows)
        c_re, c_im = cur_re[at, :], cur_im[at, :]
        r_re, r_im = rot_re[at, :], rot_im[at, :]
        cur_re[at, :] = c_re * r_re - c_im * r_im
        cur_im[at, :] = c_re * r_im + c_im * r_re
        r_re, r_im = far_re[at, :], far_im[at, :]
        for q in range(block):
            w_re[q, at, :] = c_re.astype(jnp.bfloat16)
            w_im[q, at, :] = c_im.astype(jnp.bfloat16)
            if q + 1 < block:
                c_re, c_im = c_re * r_re - c_im * r_im, c_re * r_im + c_im * r_re
        return carry

    lax.fori_loop(0, inputs // rows, advance, 0, unroll=True)

    received = bins_ref[...].astype(jnp.float32).reshape(sources * size, lanes)
    for part in range(lanes // LANES):
        rows_buf[part] = received[:, part * LANES : (part + 1) * LANES]
    mirror = jnp.where(k1 >= RADIX // 2, size // 2, 0)

    def gathered(row):
        parts = []
        for chan in range(chan_count):
            at = pl.ds(chan * tm_count * size + mirror + row, tm_count, stride=size)
            pieces = [rows_buf[part, at, :] for part in range(lanes // LANES)]
            parts.append(jnp.concatenate(pieces, axis=1))
        return jnp.concatenate(
            [
                jnp.concatenate([p[:, s * own_inputs : (s + 1) * own_inputs] for p in parts], axis=1)
                for s in range(spec_dev)
            ],
            axis=0,
        )

    g_re_all, g_im_all = gain_ref[0, :, 0], gain_ref[1, :, 0]
    for q in range(block):
        a_re, a_im = gathered(q), gathered(block + q)
        g_re, g_im = g_re_all[q], g_im_all[q]
        cal_re = (g_re * a_re - g_im * a_im).astype(jnp.bfloat16)
        cal_im = (g_re * a_im + g_im * a_re).astype(jnp.bfloat16)
        stacked = jnp.concatenate([cal_re, cal_im], axis=0)
        flipped = jnp.concatenate([cal_im, -cal_re], axis=0)
        over_time = (((0,), (0,)), ((), ()))
        for part, left in enumerate((stacked, flipped)):
            vis = lax.dot_general(left, stacked, over_time, preferred_element_type=jnp.float32)
            vis_ref[part, q, 0] = (vis * (1.0 / spectra)).astype(jnp.bfloat16)
        by_re = jnp.dot(stacked, w_re[q], preferred_element_type=jnp.float32)
        by_im = jnp.dot(stacked, w_im[q], preferred_element_type=jnp.float32)
        beam_re = by_re[:spectra] - by_im[spectra:]
        beam_im = by_re[spectra:] + by_im[:spectra]
        power = beam_re * beam_re + beam_im * beam_im
        for part in range(power.shape[1] // LANES):
            cols = slice(part * LANES, (part + 1) * LANES)
            power_buf[q, part] = power[:, cols]
            in_order = [
                power_buf[q, part, pl.ds(t, spec_dev, stride=tm_count), :] for t in range(tm_count)
            ]
            power_ref[q, 0, :, cols] = jnp.concatenate(in_order, axis=0).astype(jnp.bfloat16)


def correlate_bins(bins, beam_delays, cal_gains):
    sources, half, size, lanes = bins.shape
    _, chan_local, inputs = cal_gains.shape
    beams = beam_delays.shape[0]
    block = chan_local // RADIX
    spectra = sources * lanes // inputs
    table = pltpu.VMEM((inputs, beams), jnp.float32)
    vis, power = pl.pallas_call(
        correlate_bins_kernel,
        grid=(RADIX,),
        in_specs=[
            pl.BlockSpec(
                (sources, 1, size, lanes),
                lambda k: (0, jnp.where(k > half, RADIX - k, lax.rem(k, half)), 0, 0),
            ),
            pl.BlockSpec((2, block, 1, 1, inputs), lambda k: (0, 0, k, 0, 0)),
            pl.BlockSpec((beams, inputs), lambda k: (0, 0)),
        ],
        out_specs=[
            pl.BlockSpec((2, block, 1, inputs, inputs), lambda k: (0, 0, k, 0, 0)),
            pl.BlockSpec((block, 1, spectra, beams), lambda k: (0, k, 0, 0)),
        ],
        out_shape=[
            jax.ShapeDtypeStruct((2, block, RADIX, inputs, inputs), jnp.bfloat16),
            jax.ShapeDtypeStruct((block, RADIX, spectra, beams), jnp.bfloat16),
        ],
        scratch_shapes=[table] * 6
        + [pltpu.VMEM((block, inputs, beams), jnp.bfloat16)] * 2
        + [
            pltpu.VMEM((lanes // LANES, sources * size, LANES), jnp.float32),
            pltpu.VMEM((block, beams // LANES, spectra, LANES), jnp.float32),
        ],
        compiler_params=pltpu.CompilerParams(dimension_semantics=("arbitrary",)),
        name="correlate",
    )(bins, cal_gains.reshape(2, block, RADIX, 1, inputs), beam_delays)
    return (
        vis.reshape(2, chan_local, inputs, inputs),
        power.reshape(chan_local, spectra, beams),
    )


def correlate_kernel(
    spec_ref, gain_ref, delay_ref, vis_ref, power_ref, cur_re, cur_im, rot_re, rot_im, w_re, w_im
):
    step = pl.program_id(0)
    block = spec_ref.shape[1]
    spectra = spec_ref.shape[2]
    inputs = spec_ref.shape[3]
    beams = delay_ref.shape[0]

    @pl.when(step == 0)
    def _():
        chan_count = lax.axis_size("chan")
        first = (lax.axis_index("tm") * chan_count + lax.axis_index("chan")) * (
            block * pl.num_programs(0)
        )
        delays = delay_ref[...].T
        start = (delays * first % NFFT).astype(jnp.float32) * (2.0 * math.pi / NFFT)
        turn = delays.astype(jnp.float32) * (2.0 * math.pi / NFFT)
        norm = 1.0 / math.sqrt(inputs)
        cur_re[...] = jnp.cos(start) * norm
        cur_im[...] = -jnp.sin(start) * norm
        rot_re[...] = jnp.cos(turn)
        rot_im[...] = -jnp.sin(turn)

    rows = 16

    def advance(chunk, carry):
        at = pl.ds(pl.multiple_of(chunk * rows, rows), rows)
        c_re, c_im = cur_re[at, :], cur_im[at, :]
        r_re, r_im = rot_re[at, :], rot_im[at, :]
        for c in range(block):
            w_re[c, at, :] = c_re.astype(jnp.bfloat16)
            w_im[c, at, :] = c_im.astype(jnp.bfloat16)
            c_re, c_im = c_re * r_re - c_im * r_im, c_re * r_im + c_im * r_re
        cur_re[at, :] = c_re
        cur_im[at, :] = c_im
        return carry

    lax.fori_loop(0, inputs // rows, advance, 0, unroll=True)

    for c in range(block):
        a_re = spec_ref[0, c].astype(jnp.float32)
        a_im = spec_ref[1, c].astype(jnp.float32)
        g_re = gain_ref[0, c : c + 1, :]
        g_im = gain_ref[1, c : c + 1, :]
        cal_re = (g_re * a_re - g_im * a_im).astype(jnp.bfloat16)
        cal_im = (g_re * a_im + g_im * a_re).astype(jnp.bfloat16)
        stacked = jnp.concatenate([cal_re, cal_im], axis=0)
        flipped = jnp.concatenate([cal_im, -cal_re], axis=0)
        over_time = (((0,), (0,)), ((), ()))
        for part, left in enumerate((stacked, flipped)):
            vis = lax.dot_general(left, stacked, over_time, preferred_element_type=jnp.float32)
            vis_ref[part, c] = (vis * (1.0 / spectra)).astype(jnp.bfloat16)
        by_re = jnp.dot(stacked, w_re[c], preferred_element_type=jnp.float32)
        by_im = jnp.dot(stacked, w_im[c], preferred_element_type=jnp.float32)
        beam_re = by_re[:spectra] - by_im[spectra:]
        beam_im = by_re[spectra:] + by_im[:spectra]
        power_ref[c] = (beam_re * beam_re + beam_im * beam_im).astype(jnp.bfloat16)


def correlate(spectra, beam_delays, cal_gains):
    _, chan_local, spectra_total, inputs = spectra.shape
    beams = beam_delays.shape[0]
    block = math.gcd(chan_local, 8)
    table = pltpu.VMEM((inputs, beams), jnp.float32)
    return pl.pallas_call(
        correlate_kernel,
        grid=(chan_local // block,),
        in_specs=[
            pl.BlockSpec((2, block, spectra_total, inputs), lambda g: (0, g, 0, 0)),
            pl.BlockSpec((2, block, inputs), lambda g: (0, g, 0)),
            pl.BlockSpec((beams, inputs), lambda g: (0, 0)),
        ],
        out_specs=[
            pl.BlockSpec((2, block, inputs, inputs), lambda g: (0, g, 0, 0)),
            pl.BlockSpec((block, spectra_total, beams), lambda g: (g, 0, 0)),
        ],
        out_shape=[
            jax.ShapeDtypeStruct((2, chan_local, inputs, inputs), jnp.bfloat16),
            jax.ShapeDtypeStruct((chan_local, spectra_total, beams), jnp.bfloat16),
        ],
        scratch_shapes=[table] * 4 + [pltpu.VMEM((block, inputs, beams), jnp.bfloat16)] * 2,
        compiler_params=pltpu.CompilerParams(dimension_semantics=("arbitrary",)),
        name="correlate",
    )(spectra, cal_gains, beam_delays)


def shards(voltages, beam_delays, cal_gains):
    inp_dev = voltages.shape[0]
    spec_dev = voltages.shape[1] // NFFT
    tm_count = lax.axis_size("tm")
    chan_count = lax.axis_size("chan")
    spectra_total = spec_dev * tm_count
    halo = shifted(voltages[:, : (TAPS - 1) * NFFT].astype(jnp.bfloat16), "tm", -1)
    devices = tm_count * chan_count
    if CH % (4 * RADIX * devices) == 0:
        bins = exchange(channelize(voltages, halo, devices))
        return correlate_bins(bins, beam_delays, cal_gains)
    half = LANES // 2
    bins = channelize(voltages, halo, half).reshape(RADIX // 2, half, 2, 2, spec_dev, inp_dev)
    plain, mirror = bins[:, :, 0], bins[:, :, 1]
    bins = jnp.concatenate([plain, mirror[:1], mirror[:0:-1]], axis=0)
    packed = bins.transpose(2, 1, 0, 3, 4).reshape(2, CH, spec_dev, inp_dev)
    chan_local = CH // (tm_count * chan_count)
    reordered = packed.reshape(2, tm_count, chan_count, chan_local, spec_dev, inp_dev)
    reordered = reordered.transpose(0, 2, 1, 3, 4, 5).reshape(2, CH, spec_dev, inp_dev)
    sectioned = lax.all_to_all(reordered, "chan", split_axis=1, concat_axis=3, tiled=True)
    turned = lax.all_to_all(sectioned, "tm", split_axis=1, concat_axis=2, tiled=True)
    return correlate(turned, beam_delays, cal_gains)


def solution(mesh):
    return jax.shard_map(
        shards,
        mesh=mesh,
        in_specs=(P(("grp", "chan"), "tm"), P(), P(None, ("grp", "tm", "chan"), None)),
        out_specs=(
            P(None, ("grp", "tm", "chan"), None, None),
            P(("grp", "tm", "chan"), None, None),
        ),
        check_vma=False,
    )
```
